128 devices in a mesh: group: 8 (over z_lo, x), shard: 16 (over z_hi, y, core).
Axes of the slice: x: 4, y: 4, z: 4 (z_hi: 2, z_lo: 2; z = z_hi * 2 + z_lo), core: 2. Of those that a mesh axis runs over, the one named last changes fastest.
Arguments:
- src_emb: float32 [400, 262144], P(None, ('group', 'shard')), may hold values from -1.5 to 1.5
- src_state: float32 [262144], P(('group', 'shard')), may hold values from 0.1 to 1
- dst_emb: float32 [400, 8192], P(None, ('group', 'shard')), may hold values from -1.5 to 1.5
- dst_state: float32 [8192], P(('group', 'shard')), may hold values from 100 to 10000
- rel_table: float32 [400, 64], replicated, may hold values from -3 to 3
- rel_ids: int32 [2, 2, 8, 4], P(None, None, 'group'), may hold values from 0 to 63
- multiplicity: int32 [2, 2, 2048, 4], P(None, None, ('group', 'shard')), may hold values from 0 to 2
- neg_tile: int32 [2, 2, 2048], P(None, None, ('group', 'shard')), may hold values from 0 to 3
Outputs:
- src_out: float32 [400, 262144], P(None, ('group', 'shard'))
- src_state_out: float32 [262144], P(('group', 'shard'))
- dst_out: float32 [400, 8192], P(None, ('group', 'shard'))
- dst_state_out: float32 [8192], P(('group', 'shard'))
The draws below stay inside these ranges and needn't reach their ends.
All inputs are finite; a program needn't handle non-finite values.
Results may differ from the reference program's by a relative error of at most 0.0004.
The reference program's roundings to bfloat16 on the way count: a program that leaves them out, or rounds other values in their place, can miss the bound.
Values may be sent and summed in bfloat16 or wider, within the bound.
No kernel may reach another device: no remote copies, remote signals or barrier semaphores. Data moves between devices by JAX's collectives and lax.ppermute only.
A program may use at most 64 MiB of HBM per device.

```python
import math
import jax
import jax.numpy as jnp
from jax import lax

D = 400
SRC_DEV = 2048
POOL_DEV = 32
POOLS = 2
ROUNDS = 2
TILE = 128
NREL = 64
GROUPS = 8
SOURCES = 262144
DESTS = 8192
POOL_TILES = 4
SRC_TILES = 2048
N_GROUP = 8
N_SHARD = 16


def with_ends(result, key, low, top_value):
    extent = result.shape
    index_at = [jax.random.randint(jax.random.fold_in(key, axis), (), 0, extent[axis]) for axis in range(len(extent))]
    result = result.at[tuple(index_at)].set(low)
    longest = extent.index(max(extent))
    index_at[longest] = (index_at[longest] + 1) % extent[longest]
    return result.at[tuple(index_at)].set(top_value)


def block_scale(rng, shape, split, least, high):
    level, own = 1.0, jax.random.fold_in(rng, 6)
    for position, blocks in split:
        draws = jnp.exp(jax.random.uniform(jax.random.fold_in(own, position), (blocks,), jnp.float32, least / len(split), high / len(split)))
        level = level * jnp.repeat(draws, shape[position] // blocks).reshape([-1 if axis == position else 1 for axis in range(len(shape))])
    return level


def normal_values(own_key, extent, spread, most, shards=(), kind=jnp.bfloat16):
    gain = block_scale(own_key, extent, shards, -0.22, 0.18) if shards else 1.0
    values = jax.random.normal(own_key, extent, jnp.float32) * spread * gain
    return jnp.minimum(jnp.maximum(values, -most), most).astype(kind)


def setup_inputs(seed: int = 0) -> dict:
    key_list = jax.random.split(jax.random.key(seed), 9)
    src_emb = normal_values(key_list[0], (D, SOURCES), 0.25, 1.5, ((1, 128),), jnp.float32)
    src_state = jnp.clip(jnp.exp(math.log(1.0) - 2.3025851 * jax.random.uniform(key_list[1], (SOURCES,), jnp.float32) ** block_scale(key_list[1], (SOURCES,), ((0, 128),), -0.2, 0.2)), 0.1, 1.0)
    dst_emb = normal_values(key_list[2], (D, DESTS), 0.25, 1.5, ((1, 128),), jnp.float32)
    dst_state = jnp.clip(jnp.exp(math.log(10000.0) - 4.6051702 * jax.random.uniform(key_list[3], (DESTS,), jnp.float32) ** block_scale(key_list[3], (DESTS,), ((0, 128),), -0.2, 0.2)), 100.0, 10000.0)
    rel_table = normal_values(key_list[4], (D, NREL), 1.0, 3.0, (), jnp.float32)
    rel_ids = with_ends(jax.random.randint(key_list[5], (ROUNDS, POOLS, GROUPS, POOL_TILES), 0, NREL), jax.random.fold_in(key_list[5], 1), 0, NREL - 1).astype(jnp.int32)
    multiplicity = with_ends(jax.random.randint(key_list[6], (ROUNDS, POOLS, SRC_TILES, POOL_TILES), 0, 3), jax.random.fold_in(key_list[6], 1), 0, 2).astype(jnp.int32)
    neg_tile = with_ends(jax.random.randint(key_list[7], (ROUNDS, POOLS, SRC_TILES), 0, POOL_TILES), jax.random.fold_in(key_list[7], 1), 0, POOL_TILES - 1).astype(jnp.int32)
    return {"src_emb": src_emb, "src_state": src_state, "dst_emb": dst_emb, "dst_state": dst_state, "rel_table": rel_table, "rel_ids": rel_ids, "multiplicity": multiplicity, "neg_tile": neg_tile}


LEARN_RATE = 0.1
POSITIVE_WEIGHT = 0.125
NEGATIVE_WEIGHT = 0.25
HIGHEST_PRECISION = lax.Precision.HIGHEST

def column_tiles(offset, columns, tile_count):
    tile_of = (offset + lax.iota(jnp.int32, columns)) // TILE
    return (tile_of[None, :] == lax.iota(jnp.int32, tile_count)[:, None]).astype(jnp.float32)

def relation_columns(rel_table, rel_row, offset, columns):
    tile_count = rel_row.shape[0]
    chosen = (rel_row[None, :] == lax.iota(jnp.int32, rel_table.shape[1])[:, None]).astype(jnp.float32)
    per_tile = jnp.dot(rel_table, chosen, precision=HIGHEST_PRECISION)
    return jnp.dot(per_tile, column_tiles(offset, columns, tile_count), precision=HIGHEST_PRECISION)

def pair_gradient(scores, mult_f, neg_hot, offset, columns):
    col_tiles = column_tiles(offset, columns, mult_f.shape[1])
    positive = jnp.dot(mult_f, col_tiles, precision=HIGHEST_PRECISION)
    negative = jnp.dot(neg_hot, col_tiles, precision=HIGHEST_PRECISION)
    row_tiles = mult_f.shape[0]
    blocked = scores.reshape(row_tiles, TILE, columns)
    pair_grad = NEGATIVE_WEIGHT * negative[:, None, :] * jax.nn.sigmoid(blocked) - POSITIVE_WEIGHT * positive[:, None, :] * jax.nn.sigmoid(-blocked)
    return pair_grad.reshape(row_tiles * TILE, columns).astype(jnp.bfloat16)

def adagrad(embedding, accum, gradient):
    new_accum = accum + lax.optimization_barrier(jnp.mean(gradient * gradient, axis=0))
    return (embedding - LEARN_RATE * gradient / jnp.sqrt(new_accum)[None, :], new_accum)

def reference(src_emb, src_state, dst_emb, dst_state, rel_table, rel_ids, multiplicity, neg_tile):
    group_rows = SRC_DEV * N_SHARD
    group_tiles = group_rows // TILE
    pool_cols = POOL_DEV * N_SHARD
    tile_count = pool_cols // TILE
    sources = [src_emb[:, g * group_rows:(g + 1) * group_rows] for g in range(N_GROUP)]
    source_sums = [src_state[g * group_rows:(g + 1) * group_rows] for g in range(N_GROUP)]
    blocked = dst_emb.reshape(D, N_GROUP, N_SHARD, POOLS, POOL_DEV)
    blocked_sums = dst_state.reshape(N_GROUP, N_SHARD, POOLS, POOL_DEV)
    pools = [[blocked[:, q, :, p, :].reshape(D, pool_cols) for p in range(POOLS)] for q in range(N_GROUP)]
    pool_sums = [[blocked_sums[q, :, p, :].reshape(pool_cols) for p in range(POOLS)] for q in range(N_GROUP)]
    for rotation in range(ROUNDS):
        for group_index in range(N_GROUP):
            partition = (group_index - rotation) % N_GROUP
            for pool_index in range(POOLS):
                col_scale = relation_columns(rel_table, rel_ids[rotation, pool_index, group_index], 0, pool_cols)
                scaled = (pools[partition][pool_index] * col_scale).astype(jnp.bfloat16)
                source_bf = sources[group_index].astype(jnp.bfloat16)
                scores = lax.dot_general(source_bf, scaled, (((0,), (0,)), ((), ())), preferred_element_type=jnp.float32)
                mult_f = multiplicity[rotation, pool_index, group_index * group_tiles:(group_index + 1) * group_tiles].astype(jnp.float32)
                neg_rows = neg_tile[rotation, pool_index, group_index * group_tiles:(group_index + 1) * group_tiles]
                neg_hot = (neg_rows[:, None] == lax.iota(jnp.int32, tile_count)[None, :]).astype(jnp.float32)
                pair_grad = pair_gradient(scores, mult_f, neg_hot, 0, pool_cols)
                src_grad = lax.dot_general(scaled, pair_grad, (((1,), (1,)), ((), ())), preferred_element_type=jnp.float32)
                dest_grad = col_scale * jnp.dot(source_bf, pair_grad, preferred_element_type=jnp.float32)
                sources[group_index], source_sums[group_index] = adagrad(sources[group_index], source_sums[group_index], src_grad)
                pools[partition][pool_index], pool_sums[partition][pool_index] = adagrad(pools[partition][pool_index], pool_sums[partition][pool_index], dest_grad)
    src_out = jnp.concatenate(sources, axis=1)
    src_state_out = jnp.concatenate(source_sums, axis=0)
    dst_out = jnp.stack([jnp.stack([pools[q][p].reshape(D, N_SHARD, POOL_DEV) for p in range(POOLS)], axis=2) for q in range(N_GROUP)], axis=1).reshape(D, DESTS)
    dst_state_out = jnp.stack([jnp.stack([pool_sums[q][p].reshape(N_SHARD, POOL_DEV) for p in range(POOLS)], axis=1) for q in range(N_GROUP)], axis=0).reshape(DESTS)
    return (src_out, src_state_out, dst_out, dst_state_out)
```

```python
import functools

import jax
import jax.numpy as jnp
from jax import lax
from jax.experimental import pallas as pl
from jax.experimental.pallas import tpu as pltpu
from jax.sharding import PartitionSpec as P

POOLS = 2
ROUNDS = 2
TILE = 128
LEARN_RATE = 0.1
POSITIVE_WEIGHT = 0.125
NEGATIVE_WEIGHT = 0.25
NZ, NY, NC = 2, 4, 2
CHUNK = 512
F32, BF16, F16 = jnp.float32, jnp.bfloat16, jnp.float16


def shard_index(z, y, c):
    return (z * NY + y) * NC + c


SHARDS = [(z, y, c) for z in range(NZ) for y in range(NY) for c in range(NC)]


def swap_core(x):
    return lax.ppermute(
        x, "shard", [(shard_index(z, y, c), shard_index(z, y, 1 - c)) for z, y, c in SHARDS]
    )


def swap_z(x):
    return lax.ppermute(
        x, "shard", [(shard_index(z, y, c), shard_index(1 - z, y, c)) for z, y, c in SHARDS]
    )


def shift_y(x, steps):
    return lax.ppermute(
        x,
        "shard",
        [(shard_index(z, y, c), shard_index(z, (y + steps) % NY, c)) for z, y, c in SHARDS],
    )


def shift_group(x, steps, flip):
    groups, shards = lax.axis_size("group"), lax.axis_size("shard")
    pairs = []
    for g in range(groups):
        for z, y, c in SHARDS:
            target = shard_index(1 - z if flip else z, y, c)
            pairs.append(
                (g * shards + shard_index(z, y, c), ((g + steps) % groups) * shards + target)
            )
    return lax.ppermute(x, ("group", "shard"), pairs)


def pair_kernel(pool_ref, src_ref, tanh_ref, const_ref, pair_ref, dest_ref):
    rows = pool_ref.shape[0]
    blocks = tanh_ref.shape[0]
    each = rows // blocks
    columns = src_ref.shape[1]
    pool = pool_ref[...]
    total = None
    for start in range(0, columns, CHUNK):
        part = slice(start, start + CHUNK)
        scores = jnp.dot(pool, src_ref[:, part], preferred_element_type=F32)
        gate = jnp.tanh(0.5 * scores).reshape(blocks, each, CHUNK)
        pair = gate * tanh_ref[:, part][:, None, :] + const_ref[:, part][:, None, :]
        pair = pair.reshape(rows, CHUNK).astype(BF16)
        pair_ref[:, part] = pair
        dest = lax.dot_general(
            pair, src_ref[:, part], (((1,), (1,)), ((), ())), preferred_element_type=F32
        )
        total = dest if total is None else total + dest
    dest_ref[...] = total


def pair_step(pool, source_bf, gate_w, const_w):
    rows, width = pool.shape
    columns = source_bf.shape[1]
    vmem = pl.BlockSpec(memory_space=pltpu.VMEM)
    return pl.pallas_call(
        pair_kernel,
        out_shape=(
            jax.ShapeDtypeStruct((rows, columns), BF16),
            jax.ShapeDtypeStruct((rows, width), F32),
        ),
        in_specs=[vmem] * 4,
        out_specs=(vmem, vmem),
        compiler_params=pltpu.CompilerParams(vmem_limit_bytes=16 << 20),
        cost_estimate=pl.CostEstimate(
            flops=4 * rows * width * columns, bytes_accessed=1 << 20, transcendentals=rows * columns
        ),
        name="pair_step",
    )(pool, source_bf, gate_w, const_w)


def source_kernel(
    own_ref, other_ref, own_pair_ref, other_pair_ref, src_ref, state_ref, out_ref, sum_ref, bf_ref
):
    columns = src_ref.shape[1]
    width = src_ref.shape[0]
    own = own_ref[...].astype(F32).T.astype(BF16)
    other = other_ref[...].astype(F32).T.astype(BF16)
    for start in range(0, columns, CHUNK):
        part = slice(start, start + CHUNK)
        grad = jnp.dot(own, own_pair_ref[:, part], preferred_element_type=F32)
        grad = grad + jnp.dot(other, other_pair_ref[:, part], preferred_element_type=F32)
        accum = state_ref[:, part] + jnp.sum(grad * grad, axis=0, keepdims=True) * (1.0 / width)
        new = src_ref[:, part] - grad * (LEARN_RATE / jnp.sqrt(accum))
        out_ref[:, part] = new
        sum_ref[:, part] = accum
        bf_ref[:, part] = new.astype(BF16)


def source_step(own, other, own_pair, other_pair, src, state):
    width, columns = src.shape
    rows = own.shape[0] * 2
    vmem = pl.BlockSpec(memory_space=pltpu.VMEM)
    return pl.pallas_call(
        source_kernel,
        out_shape=(
            jax.ShapeDtypeStruct((width, columns), F32),
            jax.ShapeDtypeStruct((1, columns), F32),
            jax.ShapeDtypeStruct((width, columns), BF16),
        ),
        in_specs=[vmem] * 6,
        out_specs=(vmem, vmem, vmem),
        compiler_params=pltpu.CompilerParams(vmem_limit_bytes=24 << 20),
        cost_estimate=pl.CostEstimate(
            flops=2 * rows * width * columns, bytes_accessed=4 << 20, transcendentals=columns
        ),
        name="source_step",
    )(own, other, own_pair, other_pair, src, state)


def adagrad_rows(embedding, accum, gradient):
    new_accum = accum + jnp.mean(gradient * gradient, axis=1)
    return embedding - LEARN_RATE * gradient / jnp.sqrt(new_accum)[:, None], new_accum


def gather_y(block):
    received = [shift_y(block, steps) for steps in (1, 3, 2)]
    return jnp.concatenate([block, received[0], received[2], received[1]], axis=0)


def reduce_y(kept, sent):
    received = [shift_y(block, -k) for block, k in zip(sent, (1, 3, 2))]
    for block in received:
        kept = kept + block.astype(F32)
    return kept


def local(src_emb, src_state, dst_emb, dst_state, rel_table, rel_ids, multiplicity, neg_tile):
    width, columns = src_emb.shape
    each = dst_emb.shape[1] // POOLS
    tiles = multiplicity.shape[3]
    shard_pos = lax.axis_index("shard")
    z, y = shard_pos // (NY * NC), (shard_pos // NC) % NY

    home = dst_emb.T.reshape(POOLS, each, width)
    home_sums = dst_state.reshape(POOLS, each)

    flips = jnp.arange(NZ)
    back = jnp.arange(NY)
    per_tile = TILE // each
    tile_of = shard_index((z + flips) % NZ, (y - back[:, None]) % NY, 0) // per_tile
    own_tiles = tile_of[0]
    block_tiles = tile_of.reshape(-1)

    chosen = rel_ids[:, :, 0, :][:, :, own_tiles]
    onehot = (chosen[..., None] == jnp.arange(rel_table.shape[1])).astype(F32)
    rel_rows = lax.dot_general(
        onehot, rel_table, (((3,), (1,)), ((), ())), precision=lax.Precision.HIGHEST
    )

    first = (home * rel_rows[0, :, 0][:, None, :]).astype(BF16)
    other_z = swap_z(first)

    packed = jnp.concatenate(
        [home, jnp.broadcast_to(home_sums[:, :, None], home.shape[:2] + (112,))], axis=2
    )
    tile_hot = (block_tiles[:, None] == jnp.arange(tiles)).astype(F32)
    mult = jnp.sum(
        tile_hot[None, None, :, None, :] * multiplicity.astype(F32)[:, :, None], axis=-1
    )
    negative = (neg_tile[:, :, None, :] == block_tiles[None, None, :, None]).astype(F32)
    pull, push = NEGATIVE_WEIGHT * negative, POSITIVE_WEIGHT * mult
    spread = lambda w: jnp.repeat(w, TILE, axis=-1)
    gate_w = spread(0.5 * (pull + push))
    const_w = spread(0.5 * (pull - push))

    source_bf = src_emb.astype(BF16)
    state = src_state[None, :]
    blocks = [jnp.concatenate([first[p], other_z[p]], axis=0) for p in range(POOLS)]
    new_home, new_home_sums = [], []
    for rotation in range(ROUNDS):
        next_blocks = []
        for p in range(POOLS):
            own = gather_y(blocks[p])
            if rotation == 0 and p == 0:
                packed, _ = lax.optimization_barrier((packed, own))
                ahead = jnp.stack(
                    [shift_group(packed, 1, False), shift_group(packed, 1, True)], axis=1
                )
                ahead_emb = ahead[..., :width].reshape(POOLS, NZ * each, width)
                ahead_sums = ahead[..., width].reshape(POOLS, NZ * each)
            other = swap_core(own)
            weights = (gate_w[rotation, p], const_w[rotation, p])
            own_pair, own_dest = pair_step(own, source_bf, *weights)
            other_pair, other_dest = pair_step(other, source_bf, *weights)
            partner_dest = swap_core(other_dest)
            src_emb, state, source_bf = source_step(
                own, other, own_pair, other_pair, src_emb, state
            )
            dest = (own_dest + partner_dest).reshape(NY, NZ * each, width)
            sent = [dest[k].astype(F16) for k in (1, 3, 2)]
            kept = dest[0]
            total = reduce_y(kept, sent)
            scaled = total.reshape(NZ, each, width) * rel_rows[rotation, p][:, None, :]
            if rotation == 0:
                scaled_16 = scaled.astype(F16)
                straight = shift_group(scaled_16, 1, False).astype(F32)
                crossed = shift_group(scaled_16, 1, True).astype(F32)
                grad = straight + crossed[::-1]
                emb, _ = adagrad_rows(
                    ahead_emb[p], ahead_sums[p], grad.reshape(NZ * each, width)
                )
                emb = emb.reshape(NZ, each, width) * rel_rows[1, p][:, None, :]
                next_blocks.append(emb.astype(BF16).reshape(NZ * each, width))
                home_grad = scaled[0] + swap_z(scaled[1])
                new_home.append(adagrad_rows(home[p], home_sums[p], home_grad))
            else:
                home_grad = shift_group(scaled[0], -1, False) + shift_group(scaled[1], -1, True)
                new_home[p] = adagrad_rows(*new_home[p], home_grad)
        blocks = next_blocks
    dst_out = jnp.concatenate([emb for emb, _ in new_home], axis=0).T
    dst_sums = jnp.concatenate([sums for _, sums in new_home], axis=0)
    return src_emb, state[0], dst_out, dst_sums


def solution(mesh):
    placed = (
        P(None, ("group", "shard")),
        P(("group", "shard")),
        P(None, ("group", "shard")),
        P(("group", "shard")),
        P(),
        P(None, None, "group", None),
        P(None, None, ("group", "shard"), None),
        P(None, None, ("group", "shard")),
    )
    return jax.shard_map(
        local,
        mesh=mesh,
        in_specs=placed,
        out_specs=placed[:4],
        check_vma=False,
    )
```

```python
import functools

import jax
import jax.numpy as jnp
from jax import lax
from jax.experimental import pallas as pl
from jax.experimental.pallas import tpu as pltpu
from jax.sharding import PartitionSpec as P

POOLS = 2
ROUNDS = 2
TILE = 128
LEARN_RATE = 0.1
POSITIVE_WEIGHT = 0.125
NEGATIVE_WEIGHT = 0.25
NZ, NY, NC = 2, 4, 2
CHUNK = 512
F32, BF16, F16 = jnp.float32, jnp.bfloat16, jnp.float16


def shard_index(z, y, c):
    return (z * NY + y) * NC + c


SHARDS = [(z, y, c) for z in range(NZ) for y in range(NY) for c in range(NC)]


def swap_core(x):
    return lax.ppermute(
        x, "shard", [(shard_index(z, y, c), shard_index(z, y, 1 - c)) for z, y, c in SHARDS]
    )


def swap_z(x):
    return lax.ppermute(
        x, "shard", [(shard_index(z, y, c), shard_index(1 - z, y, c)) for z, y, c in SHARDS]
    )


def shift_y(x, steps):
    return lax.ppermute(
        x,
        "shard",
        [(shard_index(z, y, c), shard_index(z, (y + steps) % NY, c)) for z, y, c in SHARDS],
    )


def shift_group(x, steps, flip):
    groups, shards = lax.axis_size("group"), lax.axis_size("shard")
    pairs = []
    for g in range(groups):
        for z, y, c in SHARDS:
            target = shard_index(1 - z if flip else z, y, c)
            pairs.append(
                (g * shards + shard_index(z, y, c), ((g + steps) % groups) * shards + target)
            )
    return lax.ppermute(x, ("group", "shard"), pairs)


def call(kernel, outs, *args, vmem=8, flops=0, smem=(), aliases=None, name=None):
    specs = [
        pl.BlockSpec(memory_space=pltpu.SMEM if i in smem else pltpu.VMEM)
        for i in range(len(args))
    ]
    moved = sum(a.size * a.dtype.itemsize for a in args)
    return pl.pallas_call(
        kernel,
        out_shape=outs,
        in_specs=specs,
        out_specs=jax.tree.map(lambda _: pl.BlockSpec(memory_space=pltpu.VMEM), outs),
        input_output_aliases=aliases or {},
        compiler_params=pltpu.CompilerParams(vmem_limit_bytes=vmem << 20),
        cost_estimate=pl.CostEstimate(flops=flops, bytes_accessed=moved, transcendentals=0),
        name=name,
    )(*args)


def position():
    shard = lax.axis_index("shard")
    return shard // (NY * NC), (shard // NC) % NY


def column(row):
    count = row.shape[1]
    return jnp.broadcast_to(row, (count, count)).T[:, :1]


def pack_kernel(emb_ref, sums_ref, out_ref):
    rows = emb_ref.shape[0]
    out_ref[:rows] = emb_ref[...]
    out_ref[rows:] = jnp.zeros_like(out_ref[rows:])
    out_ref[rows:, :rows] = jnp.broadcast_to(sums_ref[...], (out_ref.shape[0] - rows, rows))


def relation_kernel(per_tile, each, ids_ref, table_ref, out_ref, spread_ref):
    z, y = position()
    for rotation in range(ROUNDS):
        for p in range(POOLS):
            for flip in range(NZ):
                tile = shard_index(z + flip - 2 * z * flip, y, 0) // per_tile
                chosen = table_ref[pl.ds(ids_ref[rotation, p, 0, tile], 1), :]
                row = (rotation * POOLS + p) * NZ + flip
                out_ref[row : row + 1, :] = chosen
                first = (flip * POOLS + p) * each
                spread_ref[rotation, first : first + each] = jnp.broadcast_to(
                    chosen, (each, chosen.shape[1])
                )


def scale_pool(values, rel, rotation, flip):
    each = values.shape[0] // POOLS
    first = (rotation * POOLS) * NZ + flip
    return jnp.concatenate(
        [
            values[p * each : (p + 1) * each] * rel[first + p * NZ : first + p * NZ + 1]
            for p in range(POOLS)
        ],
        axis=0,
    )


def scale_kernel(own_ref, other_ref, rel_ref, block_ref, both_ref):
    rows = block_ref.shape[0] // NZ
    rel = rel_ref[...]
    for flip, ref in enumerate((own_ref, other_ref)):
        scaled = scale_pool(ref[:rows], rel, 0, flip)
        block_ref[flip * rows : (flip + 1) * rows] = scaled.astype(BF16)
        both_ref[flip] = ref[...]


def update(emb, sums, grad):
    mean = jnp.sum(grad * grad, axis=1, keepdims=True) * (1.0 / grad.shape[1])
    accum = sums + mean
    return emb - LEARN_RATE * grad / jnp.sqrt(accum), accum


def ahead_kernel(ahead_ref, grad_ref, rel_ref, block_ref):
    rows = grad_ref.shape[0] // NZ
    rel = rel_ref[...]
    for flip in range(NZ):
        part = slice(flip * rows, (flip + 1) * rows)
        sums = column(ahead_ref[flip, rows : rows + 1, :rows])
        emb, _ = update(ahead_ref[flip, :rows], sums, grad_ref[part])
        block_ref[part] = scale_pool(emb, rel, 1, flip).astype(BF16)


def home_kernel(emb_ref, sums_ref, kept_ref, met_ref, left_ref, right_ref, out_ref, new_ref):
    emb, sums = update(emb_ref[...], column(sums_ref[...]), kept_ref[...] + met_ref[...])
    emb, sums = update(emb, sums, left_ref[...] + right_ref[...])
    out_ref[...] = emb
    rows = sums.shape[0]
    new_ref[...] = jnp.broadcast_to(sums, (rows, rows)).T[:1]


def pair_kernel(step, per_tile, pool_ref, src_ref, gate_ref, const_ref, pair_ref, dest_ref):
    width = pool_ref.shape[-1]
    rows = pair_ref.shape[0]
    blocks = NY * NZ
    each = rows // blocks
    columns = src_ref.shape[1]
    tiles = gate_ref.shape[0] // (ROUNDS * POOLS)
    z, y = position()
    pool = pool_ref[:, :, step % POOLS].reshape(rows, width)
    lines = []
    for back in range(NY):
        for flip in range(NZ):
            there = jnp.bitwise_and(y - back + NY, NY - 1)
            lines.append(
                step * tiles + shard_index(z + flip - 2 * z * flip, there, 0) // per_tile
            )
    total = None
    for start in range(0, columns, CHUNK):
        part = slice(start, start + CHUNK)
        scores = jnp.dot(pool, src_ref[:, part], preferred_element_type=F32)
        gate = jnp.tanh(0.5 * scores)
        pair = jnp.concatenate(
            [
                gate[b * each : (b + 1) * each] * gate_ref[pl.ds(line, 1), part]
                + const_ref[pl.ds(line, 1), part]
                for b, line in enumerate(lines)
            ],
            axis=0,
        ).astype(BF16)
        pair_ref[:, part] = pair
        dest = lax.dot_general(
            pair, src_ref[:, part], (((1,), (1,)), ((), ())), preferred_element_type=F32
        )
        total = dest if total is None else total + dest
    dest_ref[...] = total


def pair_step(step, per_tile, pools, source_bf, gate_w, const_w):
    width, columns = source_bf.shape
    rows = pools.size // (POOLS * width)
    return call(
        functools.partial(pair_kernel, step, per_tile),
        (jax.ShapeDtypeStruct((rows, columns), BF16), jax.ShapeDtypeStruct((rows, width), F32)),
        pools,
        source_bf,
        gate_w,
        const_w,
        vmem=16,
        flops=4 * rows * width * columns,
        name="pair_step",
    )


def source_kernel(
    pool_index,
    own_ref,
    other_ref,
    own_pair_ref,
    other_pair_ref,
    src_ref,
    state_ref,
    out_ref,
    sum_ref,
    bf_ref=None,
):
    width, columns = src_ref.shape
    rows = own_pair_ref.shape[0]
    own, other = (
        ref[:, :, pool_index].reshape(rows, width).astype(F32).T.astype(BF16)
        for ref in (own_ref, other_ref)
    )
    for start in range(0, columns, CHUNK):
        part = slice(start, start + CHUNK)
        grad = jnp.dot(own, own_pair_ref[:, part], preferred_element_type=F32)
        grad = grad + jnp.dot(other, other_pair_ref[:, part], preferred_element_type=F32)
        accum = state_ref[:, part] + jnp.sum(grad * grad, axis=0, keepdims=True) * (1.0 / width)
        new = src_ref[:, part] - grad * (LEARN_RATE / jnp.sqrt(accum))
        out_ref[:, part] = new
        sum_ref[:, part] = accum
        if bf_ref is not None:
            bf_ref[:, part] = new.astype(BF16)


def source_step(pool_index, own, other, own_pair, other_pair, src, state, last):
    width, columns = src.shape
    rows = own_pair.shape[0] * 2
    outs = [
        jax.ShapeDtypeStruct((width, columns), F32),
        jax.ShapeDtypeStruct((1, columns), F32),
        jax.ShapeDtypeStruct((width, columns), BF16),
    ]
    result = call(
        functools.partial(source_kernel, pool_index),
        outs[:2] if last else outs,
        own,
        other,
        own_pair,
        other_pair,
        src,
        state,
        vmem=16,
        flops=2 * rows * width * columns,
        name="source_step",
    )
    return (*result, None) if last else result


def combine_kernel(*refs):
    dests, outs = refs[: 2 * POOLS], refs[2 * POOLS :]
    each = dests[0].shape[0] // (NY * NZ)
    for k, ref in enumerate(outs):
        for flip in range(NZ):
            for p in range(POOLS):
                there = (flip * POOLS + p) * each
                part = slice((k * NZ + flip) * each, (k * NZ + flip + 1) * each)
                ref[there : there + each] = dests[2 * p][part] + dests[2 * p + 1][part]


def gather_y(block):
    received = {steps: shift_y(block, steps) for steps in (2, 1, 3)}
    return jnp.stack([block, received[1], received[2], received[3]], axis=0)


def local(src_emb, src_state, dst_emb, dst_state, rel_table, rel_ids, multiplicity, neg_tile):
    width, columns = src_emb.shape
    rows = dst_emb.shape[1]
    each = rows // POOLS
    tiles = multiplicity.shape[3]
    per_tile = TILE // each
    steps = ROUNDS * POOLS
    shaped = jax.ShapeDtypeStruct

    home = dst_emb.T
    home_sums = dst_state[None, :]
    packed = call(pack_kernel, shaped((rows + 8, width), F32), home, home_sums, name="pack")
    other_packed = swap_z(packed)
    rel, rel_spread = call(
        functools.partial(relation_kernel, per_tile, each),
        (shaped((steps * NZ, width), F32), shaped((ROUNDS, NZ * rows, width), F32)),
        rel_ids,
        rel_table.T,
        smem=(0,),
        name="relations",
    )
    block, both = call(
        scale_kernel,
        (shaped((NZ * rows, width), BF16), shaped((NZ, rows + 8, width), F32)),
        packed,
        other_packed,
        rel,
        name="scale",
    )
    block, src_bf_in, multiplicity, neg_tile = lax.optimization_barrier(
        (block, src_emb, multiplicity, neg_tile)
    )

    pull = NEGATIVE_WEIGHT * (
        neg_tile[:, :, None, :] == jnp.arange(tiles)[None, None, :, None]
    ).astype(F32)
    push = POSITIVE_WEIGHT * multiplicity.transpose(0, 1, 3, 2).astype(F32)
    spread = lambda w: jnp.repeat(w.reshape(steps * tiles, -1), TILE, axis=-1)
    gate_w = spread(0.5 * (pull + push))
    const_w = spread(0.5 * (pull - push))

    source_bf = src_bf_in.astype(BF16)
    state = src_state[None, :]
    for rotation in range(ROUNDS):
        own = gather_y(block)
        if rotation == 0:
            ahead, own = lax.optimization_barrier((shift_group(both, 1, False), own))
        else:
            home_sent, own = lax.optimization_barrier((home_sent, own))
            home_met = swap_z(home_sent)
        own = own.reshape(NY, NZ, POOLS, each, width)
        other = swap_core(own)
        dests = []
        for p in range(POOLS):
            step = rotation * POOLS + p
            pools = (own, other) if p == 0 else (other, own)
            pairs = []
            for half in pools:
                pairs.append(pair_step(step, per_tile, half, source_bf, gate_w, const_w))
                if half is other:
                    partner_dest = swap_core(pairs[-1][1])
            (own_pair, own_dest), (other_pair, _) = pairs if p == 0 else pairs[::-1]
            dests += [own_dest, partner_dest]
            if p == POOLS - 1:
                piece = shaped((NZ * rows, width), F32)
                kept, *sent = call(combine_kernel, [piece] * NY, *dests, name="combine")
                sent = {k: sent[k - 1].astype(F16) for k in range(1, NY)}
                own_pair, kept, sent = lax.optimization_barrier((own_pair, kept, sent))
            src_emb, state, source_bf = source_step(
                p, own, other, own_pair, other_pair, src_emb, state, step == steps - 1
            )
        received = [shift_y(sent[k], -k) for k in (2, 1, 3)]
        received[2], src_emb, state = lax.optimization_barrier((received[2], src_emb, state))
        for piece in received:
            kept = kept + piece.astype(F32)
        scaled = kept * rel_spread[rotation]
        if rotation == 0:
            scaled_16 = scaled.astype(F16)
            straight = shift_group(scaled_16, 1, False)
            crossed = shift_group(scaled_16, 1, True)
            grad = straight.astype(F32) + jnp.concatenate(
                [crossed[rows:], crossed[:rows]], axis=0
            ).astype(F32)
            block = call(
                ahead_kernel, shaped((NZ * rows, width), BF16), ahead, grad, rel, name="ahead"
            )
            home_kept, home_sent = scaled[:rows], scaled[rows:]
        else:
            left = shift_group(scaled[:rows], -1, False)
            right = shift_group(scaled[rows:], -1, True)
    out, sums = call(
        home_kernel,
        (shaped((rows, width), F32), shaped((1, rows), F32)),
        home,
        home_sums,
        home_kept,
        home_met,
        left,
        right,
        name="home",
    )
    return src_emb, state[0], out.T, sums[0]


def solution(mesh):
    placed = (
        P(None, ("group", "shard")),
        P(("group", "shard")),
        P(None, ("group", "shard")),
        P(("group", "shard")),
        P(),
        P(None, None, "group", None),
        P(None, None, ("group", "shard"), None),
        P(None, None, ("group", "shard")),
    )
    return jax.shard_map(
        local,
        mesh=mesh,
        in_specs=placed,
        out_specs=placed[:4],
        check_vma=False,
    )
```
